512 devices in a mesh: gx: 8 (over y, core), yz: 64 (over x, z).
Axes of the slice: x: 4, y: 4, z: 16, core: 2. Of those that a mesh axis runs over, the one named last changes fastest.
Arguments:
- elem_tiles: bfloat16 [8192, 36864], P(('gx', 'yz')), may hold values from -0.0390625 to 0.0390625
- inv_factor: bfloat16 [1024, 36864], P(('gx', 'yz'))
- rhs: bfloat16 [1024, 192, 128], P(('gx', 'yz')), may hold values from -6 to 6
- mig_source: int32 [8, 128], P('gx'), may hold values from 0 to 127, as said below
- tile_target: int32 [8, 1024], P('gx'), may hold values from 0 to 1023, as said below
- col_index: int32 [1024, 8], P(('gx', 'yz')), may hold values from 0 to 5
Outputs:
- iterate: float32 [1024, 192, 128], P(('gx', 'yz'))
The draws below stay inside these ranges and needn't reach their ends.
Inputs may be any that keep to these rules, and one draw needn't show every extreme that they name: `mig_source`: each slab's row is a permutation. A block moves only between owners whose indices differ in the highest bit (index and index + 32) or in the lowest bit (index and index xor 1), at most one block from a device for each of these two bits; every draw moves a block between owners 0 and 32 of each slab. `tile_target`: each slab's row is a permutation. Element tile t of owner a goes to owner (a + s_t) mod 64, with shifts s_t common to a slab's owners, one of them 64/2; at most 1 tiles go from one owner to one owner, and that many do from every owner.
All inputs are finite; a program needn't handle non-finite values.
Results may differ from the reference program's by a relative error of at most 0.0033.
Values may be sent and summed in bfloat16 or wider, within the bound.
A program may use at most 128 MiB of HBM per device.

```python
import jax
import jax.numpy as jnp
from jax import lax

BS = 192
NNZ = 8
HB = 2
ITERS = 3
RB = 2
NRHS = 128
TD = 16
CAP_T = 1
OWNERS = 64
SLABS = 8
SLAB_BLK = 128
SLAB_TILES = 1024
NBLK = 1024


def draw_inv_factor(key, part):
    flat_ids = jnp.arange(BS * BS, dtype=jnp.int32)
    unit_diag = (flat_ids // BS == flat_ids % BS).astype(jnp.float32)
    spread = jax.random.normal(key, (NBLK, BS * BS), jnp.float32) * (0.25 / BS ** 0.5)
    return (unit_diag[None, :] + spread).astype(jnp.bfloat16)


def draw_mig_source(key, part):
    log_owners = OWNERS.bit_length() - 1
    bit_total = min(log_owners, RB)

    def one_slab(slab_key):
        key_hot, key_coin, key_slot = jax.random.split(slab_key, 3)
        eroded = jax.random.randint(key_hot, (OWNERS,), 0, 100) < 20
        coin_flip = jax.random.randint(key_coin, (max(bit_total, 1), OWNERS), 0, 2)
        slot_order = jax.vmap(lambda one_key: jax.random.permutation(one_key, RB))(jax.random.split(key_slot, OWNERS))
        device_ids = jnp.arange(OWNERS, dtype=jnp.int32)
        source_map = device_ids[:, None] * RB + jnp.arange(RB, dtype=jnp.int32)[None, :]
        for step_index in range(bit_total):
            bit_index = log_owners - 1 if step_index == 0 else step_index - 1
            partner = jnp.bitwise_xor(device_ids, 1 << bit_index)
            lowest = jnp.minimum(device_ids, partner)
            swapped = (eroded | eroded[partner]) & (coin_flip[step_index, lowest] == 1)
            if step_index == 0:
                swapped = swapped | (lowest == 0)
            slot_mine = slot_order[:, step_index]
            slot_theirs = slot_order[partner, step_index]
            fresh = partner * RB + slot_theirs
            source_map = source_map.at[device_ids, slot_mine].set(jnp.where(swapped, fresh, source_map[device_ids, slot_mine]))
        return source_map.reshape(-1).astype(jnp.int32)
    return jax.vmap(one_slab)(jax.random.split(key, SLABS))


def draw_tile_target(key, part):

    def one_slab(slab_key):
        key_shift, key_slot = jax.random.split(slab_key)
        order_ids = jax.random.permutation(key_shift, CAP_T * OWNERS)
        shifts = (order_ids[:TD] - order_ids[0] + OWNERS // 2) % OWNERS
        slot_perm = jax.vmap(lambda one_key: jax.random.permutation(one_key, TD))(jax.random.split(key_slot, OWNERS))
        owner_ids = jnp.arange(OWNERS, dtype=jnp.int32)[:, None]
        tile_ids = jnp.arange(TD, dtype=jnp.int32)[None, :]
        dest_dev = (owner_ids + shifts[None, :]) % OWNERS
        dest_slot = slot_perm[dest_dev, tile_ids]
        return (dest_dev * TD + dest_slot).reshape(-1).astype(jnp.int32)
    return jax.vmap(one_slab)(jax.random.split(key, SLABS))


def touch_ends(entries, key, least, largest):
    extent = entries.shape
    spot = [jax.random.randint(jax.random.fold_in(key, axis), (), 0, extent[axis]) for axis in range(len(extent))]
    entries = entries.at[tuple(spot)].set(least)
    longest = extent.index(max(extent))
    spot[longest] = (spot[longest] + 1) % extent[longest]
    return entries.at[tuple(spot)].set(largest)


def levels(rng, extent, cuts, low, high):
    loudness, own = 1.0, jax.random.fold_in(rng, 6)
    for position, parts in cuts:
        steps = jnp.exp(jax.random.uniform(jax.random.fold_in(own, position), (parts,), jnp.float32, low / len(cuts), high / len(cuts)))
        loudness = loudness * jnp.repeat(steps, extent[position] // parts).reshape([-1 if axis == position else 1 for axis in range(len(extent))])
    return loudness


def centred(rng, dims, width, bound, pieces=(), held_as=jnp.bfloat16):
    drawn = width * jax.random.normal(rng, dims, jnp.float32)
    if pieces:
        drawn = drawn * levels(rng, dims, pieces, -0.22, 0.18)
    return jnp.clip(drawn, -bound, bound).astype(held_as)


def setup_inputs(seed: int = 0) -> dict:
    key_list = jax.random.split(jax.random.key(seed), 7)
    return {
        "elem_tiles": centred(key_list[0], (SLABS * SLAB_TILES, BS * BS), (16 * NNZ * BS) ** -0.5, 0.0390625, ((0, 512),)),
        "inv_factor": draw_inv_factor(jax.random.fold_in(key_list[6], 71), 0),
        "rhs": centred(key_list[2], (NBLK, BS, NRHS), 1.0, 6.0, ((0, 512),)),
        "mig_source": draw_mig_source(jax.random.fold_in(key_list[6], 71), 0),
        "tile_target": draw_tile_target(jax.random.fold_in(key_list[6], 71), 0),
        "col_index": touch_ends(jax.random.randint(key_list[5], (NBLK, NNZ), 0, RB + 2 * HB), jax.random.fold_in(key_list[5], 1), 0, (RB + 2 * HB) - 1).astype(jnp.int32),
    }


def apply_factor(factor_set, vector_set):
    return jnp.einsum("rij,rjn->rin", factor_set.astype(jnp.float32), vector_set.astype(jnp.float32))


def reference(elem_tiles, inv_factor, rhs, mig_source, tile_target, col_index):
    devices = SLABS * OWNERS
    slab_tiles = elem_tiles.reshape(SLABS, SLAB_TILES, BS * BS)
    slab_ids = jnp.arange(SLABS, dtype=jnp.int32)[:, None]
    tile_ids = jnp.broadcast_to(jnp.arange(SLAB_TILES, dtype=jnp.int32)[None, :], (SLABS, SLAB_TILES))
    inverse = jnp.zeros((SLABS, SLAB_TILES), jnp.int32).at[slab_ids, tile_target].set(tile_ids)
    row_tiles = jnp.take_along_axis(slab_tiles, inverse[:, :, None], axis=1).reshape(devices, RB, NNZ, BS, BS)
    factors = jnp.take_along_axis(inv_factor.reshape(SLABS, SLAB_BLK, BS * BS), mig_source[:, :, None], axis=1)
    factors = factors.reshape(devices, RB, BS, BS)
    load_cases = rhs.reshape(devices, RB, BS, NRHS)
    columns = col_index.reshape(devices, RB, NNZ)

    def precondition(vectors):
        return lax.map(lambda item_pair: apply_factor(item_pair[0], item_pair[1]), (factors, vectors))

    def one_device(entry_set):
        tile_set, col_ids, vector_set = entry_set
        picked = vector_set[col_ids]
        return jnp.einsum("rkij,rkjn->rin", tile_set.astype(jnp.float32), picked.astype(jnp.float32))

    iterate = precondition(load_cases)
    for sweep_index in range(ITERS):
        rounded = iterate.astype(jnp.bfloat16)
        slab_grid = rounded.reshape(SLABS, OWNERS, RB, BS, NRHS)
        zero_rim = jnp.zeros((1, OWNERS, HB, BS, NRHS), jnp.bfloat16)
        below_rim = jnp.concatenate([zero_rim, slab_grid[:-1, :, RB - HB:]], axis=0)
        above_rim = jnp.concatenate([slab_grid[1:, :, :HB], zero_rim], axis=0)
        padded = jnp.concatenate([below_rim, slab_grid, above_rim], axis=2).reshape(devices, RB + 2 * HB, BS, NRHS)
        applied = rounded.astype(jnp.float32) + lax.map(one_device, (row_tiles, columns, padded))
        residual = (load_cases.astype(jnp.float32) - applied).astype(jnp.bfloat16)
        iterate = iterate + precondition(residual)
    return iterate.reshape(NBLK, BS, NRHS)
```

```python
import functools

import jax
import jax.numpy as jnp
from jax import lax
from jax.experimental import pallas as pl
from jax.experimental.pallas import tpu as pltpu
from jax.sharding import PartitionSpec as P

MESH = pl.DeviceIdType.MESH
ITERS = 3
NX, NZ = 4, 16
NO = NX * NZ
T = 16
RB = 2
NK = 8
BS = 192
ROWS = BS * BS // 128
HALF = ROWS // 2
TRI = BS // 2
LANES = 4
PADX = 64
VMEM_LIMIT = 64_000_000


def prep_kernel(R, tmap, mig, elem, inv, route, cls, tiles, own, moved, wide, wide2, sz, srt, cnt, dist, off):
    my = lax.axis_index("yz")
    z = lax.rem(my, NZ)

    @pl.loop(0, TRI)
    def _(j):
        for k in range(3):
            at = pl.ds(pl.multiple_of((3 * j + k) * 128, 128), 128)
            wide[pl.ds(k * TRI + j, T, stride=ROWS), :] = elem[:, at].astype(jnp.float32)
            wide2[pl.ds(k * TRI + j, RB, stride=ROWS), :] = inv[:, at].astype(jnp.float32)

    @pl.loop(0, T)
    def _(t):
        tiles[t] = wide[pl.ds(pl.multiple_of(t * ROWS, ROWS), ROWS), :].astype(jnp.bfloat16)

    for b in range(RB):
        own[b] = wide2[pl.ds(b * ROWS, ROWS), :].astype(jnp.bfloat16)

    for n, bit in enumerate((NO // 2, 1)):
        q = jnp.bitwise_xor(my, bit)
        b = jnp.int32(0)
        for r in range(RB):
            src = mig[0, q * RB + r]
            b = jnp.where(src // RB == my, lax.rem(src, RB), b)
        moved[n] = own[b]
    for r in range(RB):
        src = mig[0, my * RB + r]
        home = src // RB
        cls[6, r] = jnp.where(
            home == my, lax.rem(src, RB), jnp.where(home == jnp.bitwise_xor(my, NO // 2), 2, 3)
        )

    @pl.loop(0, NZ)
    def _(v):
        cnt[v] = 0

    @pl.loop(0, T)
    def _(t):
        s = tmap[0, t] // T
        along = lax.rem(s, NZ)
        sz[t] = along
        cnt[along] = cnt[along] + 1
        across = s // NZ
        cls[0, t] = lax.rem(across + jnp.where(z + along >= NZ, 1, 0), NX)
        cls[1, t] = lax.rem(across + jnp.where(z < along, 1, 0), NX)
        a = lax.rem(my - s + NO, NO)
        cls[5, lax.rem(tmap[0, a * T + t], T)] = t

    def prefix(v, run):
        n = cnt[v]
        cnt[v] = run
        return run + n

    lax.fori_loop(0, NZ, prefix, jnp.int32(0))

    def place(t, far):
        v = sz[t]
        srt[cnt[v]] = t
        cnt[v] = cnt[v] + 1
        return far + NZ - v

    far = lax.fori_loop(0, T, place, jnp.int32(0))

    def split(i, c):
        up, down, best, m = c
        v = sz[srt[i]]
        up, down = up + v, down - (NZ - v)
        worst = jnp.maximum(up, down)
        better = worst < best
        return up, down, jnp.where(better, worst, best), jnp.where(better, i + 1, m)

    zero = jnp.int32(0)
    m = lax.fori_loop(0, T, split, (zero, far, far, zero))[3]

    @pl.loop(0, 2 * LANES * R)
    def _(p):
        route[0, p] = 0
        route[1, p] = 0
        route[2, p] = 0

    def plan(i, ends):
        up, down = ends
        t = srt[i]
        v = sz[t]
        goes_up = i < m
        d = jnp.where(goes_up, v, NZ - v)
        base = jnp.where(goes_up, 0, LANES * R)
        c = jnp.where(goes_up, up, down)
        last = c + d - 1
        lane0, lane1 = c // R, last // R

        @pl.when(d == 0)
        def _():
            cls[2, t] = 0
            cls[3, t] = 1

        @pl.when(d > 0)
        def _():
            cls[3, t] = 0

            @pl.when(lane0 == lane1)
            def _():
                route[0, base + c] = 1
                route[1, base + c] = t
                cls[2, t] = base + last

            @pl.when(lane0 != lane1)
            def _():
                route[0, base + lane1 * R] = 1
                route[1, base + lane1 * R] = t
                route[0, base + c] = 2
                route[2, base + last] = 1
                cls[2, t] = base + lane1 * R - 1

        return up + jnp.where(goes_up, d, 0), down + jnp.where(goes_up, 0, d)

    lax.fori_loop(0, T, plan, (zero, zero))


def main_kernel(
    R, route, cls, col, tiles, own, moved, rhs, out,
    recv1, recv2, send1, send2, save, xp1, xm1, xf1, xp2, xm2, xf2, init2, stage, rowt,
    got, fac, pad0, pad1, pad2, vec, mix, it,
    zr1, zr2, zs1, zs2, xr1, xr2, xs1, xs2, mr, ms, hr, hs,
):
    g = lax.axis_index("gx")
    slabs = lax.axis_size("gx")
    my = lax.axis_index("yz")
    x, z = my // NZ, lax.rem(my, NZ)
    line = x * NZ
    z_to = ({"yz": line + lax.rem(z + 1, NZ)}, {"yz": line + lax.rem(z + NZ - 1, NZ)})
    x_to = ({"yz": lax.rem(x + 1, NX) * NZ + z}, {"yz": lax.rem(x + NX - 1, NX) * NZ + z})
    m_to = ({"yz": lax.rem(x + NX // 2, NX) * NZ + z}, {"yz": my + 1 - 2 * lax.rem(my, 2)})
    g_to = ({"gx": lax.rem(g + 1, slabs)}, {"gx": lax.rem(g + slabs - 1, slabs)})
    pads = (pad0, pad1, pad2)

    def remote(src, dst, send, recv, to):
        return pltpu.make_async_remote_copy(
            src_ref=src, dst_ref=dst, send_sem=send, recv_sem=recv, device_id=to, device_id_type=MESH
        )

    barrier = pltpu.get_barrier_semaphore()
    greet = (*z_to, *x_to, m_to[0], *g_to)
    for to in greet:
        pl.semaphore_signal(barrier, inc=1, device_id=to, device_id_type=MESH)
    pl.semaphore_wait(barrier, len(greet))

    def moves():
        return [remote(moved.at[n], got.at[n], ms.at[n], mr.at[n], m_to[n]) for n in range(2)]

    for c in moves():
        c.start()

    for buf in (*pads, vec):
        n = buf.shape[0]
        buf[:, 0:PADX, :] = jnp.zeros((n, PADX, 128), jnp.bfloat16)
        buf[:, PADX + BS:, :] = jnp.zeros((n, PADX, 128), jnp.bfloat16)
    save[...] = jnp.zeros_like(save)

    lanes = [(d, j) for j in reversed(range(LANES)) for d in range(2)]

    def z_copy(recv, sendb, zr, zs, d, j, r):
        p = (d * LANES + j) * R + r
        k = (d * LANES + j) * 2 + lax.rem(r, 2)
        return remote(sendb.at[k], recv.at[p], zs.at[k], zr.at[p], z_to[d])

    def x_first(src, xp, xm, xr, xs, t, d):
        return remote(src.at[t], (xp, xm)[d].at[t], xs.at[d * T + t], xr.at[d * T + t], x_to[d])

    def x_second(xp, xm, xf, xr, xs, t, odd):
        src = (xm if odd else xp).at[t]
        return remote(src, xf.at[t], xs.at[2 * T + t], xr.at[2 * T + t], x_to[1 if odd else 0])

    def phase(first, x_src, recv, sendb, zr, zs, xp, xm, xf, xr, xs, between):
        pend = None
        for d, j in lanes:
            k = (d * LANES + j) * 2
            sendb[k] = first(route[1, (d * LANES + j) * R])
            if pend is not None:
                pend.start()
            pend = z_copy(recv, sendb, zr, zs, d, j, 0)
        pend.start()

        @pl.loop(0, T)
        def _(t):
            for d in range(2):
                x_first(x_src, xp, xm, xr, xs, t, d).start()

        if between is not None:
            between()

        @pl.loop(1, R)
        def _(r):
            pend = None
            for d, j in lanes:
                p = (d * LANES + j) * R + r
                z_copy(recv, sendb, zr, zs, d, j, r - 1).wait_recv()
                come = recv[p - 1]
                if j > 0:
                    s = d * LANES + j
                    save[s] = lax.select(route[2, p - 1] == 1, come, save[s])
                mode = route[0, p]
                new = first(route[1, p])
                if j < LANES - 1:
                    new = lax.select(mode == 2, save[d * LANES + j + 1], new)
                new = lax.select(mode == 0, come, new)

                @pl.when(r >= 2)
                def _():
                    z_copy(recv, sendb, zr, zs, d, j, r - 2).wait_send()

                sendb[(d * LANES + j) * 2 + lax.rem(r, 2)] = new
                if pend is not None:
                    pend.start()
                pend = z_copy(recv, sendb, zr, zs, d, j, r)
            pend.start()

            @pl.when(r <= T // 2)
            def _():
                t = 2 * (r - 1)
                x_first(x_src, xp, xm, xr, xs, t, 0).wait_recv()
                x_second(xp, xm, xf, xr, xs, t, False).start()
                x_first(x_src, xp, xm, xr, xs, t + 1, 1).wait_recv()
                x_second(xp, xm, xf, xr, xs, t + 1, True).start()

        @pl.loop(0, T // 2)
        def _(h):
            t = 2 * h
            x_first(x_src, xp, xm, xr, xs, t, 0).wait_send()
            x_first(x_src, xp, xm, xr, xs, t, 1).wait()
            x_first(x_src, xp, xm, xr, xs, t + 1, 0).wait()
            x_first(x_src, xp, xm, xr, xs, t + 1, 1).wait_send()
            for c in (x_second(xp, xm, xf, xr, xs, t, False), x_second(xp, xm, xf, xr, xs, t + 1, True)):
                c.wait()

        for d, j in lanes:
            last = z_copy(recv, sendb, zr, zs, d, j, R - 1)
            last.wait()
            z_copy(recv, sendb, zr, zs, d, j, R - 2).wait_send()

    def of_four(n, a, b, c, d):
        return lax.select(n == 0, a, lax.select(n == 1, b, lax.select(n == 2, c, d)))

    phase(
        lambda t: tiles[t, HALF:, :], tiles.at[:, 0:HALF, :], recv1, send1, zr1, zs1,
        xp1, xm1, xf1, xr1, xs1, None,
    )

    @pl.loop(0, T)
    def _(t):
        stage[t] = lax.select(cls[3, t] == 1, tiles[t, HALF:, :], recv1[cls[2, t]])
        init2[t] = of_four(cls[0, t], tiles[t, 0:HALF, :], xp1[t], xf1[t], xm1[t])

    def product(m, v):
        f0, f1, f2 = m[0:TRI], m[TRI:2 * TRI], m[2 * TRI:]
        even = jnp.dot(
            jnp.concatenate([f0, f1], axis=1), v[PADX:, :], preferred_element_type=jnp.float32
        )
        odd = jnp.dot(
            jnp.concatenate([f1, f2], axis=1), v[:PADX + BS, :], preferred_element_type=jnp.float32
        )
        return even, odd

    def halo(s):
        b = pads[s]
        mine = b.at[RB:2 * RB, PADX:PADX + BS, :]
        return (
            remote(mine, b.at[0:RB, PADX:PADX + BS, :], hs.at[2 * s], hr.at[2 * s], g_to[0]),
            remote(mine, b.at[2 * RB:, PADX:PADX + BS, :], hs.at[2 * s + 1], hr.at[2 * s + 1], g_to[1]),
        )

    def spread(ref, r, even, odd):
        ref[pl.ds(r * BS, TRI, stride=2), :] = even
        ref[pl.ds(r * BS + 1, TRI, stride=2), :] = odd

    def begin():
        for c in moves():
            c.wait()
        for r in range(RB):
            fac[r] = of_four(cls[6, r], own[0], own[1], got[0], got[1])
            vec[r, PADX:PADX + BS, :] = rhs[r]
        for r in range(RB):
            even, odd = product(fac[r], vec[r])
            spread(it, r, even, odd)
        for r in range(RB):
            pads[0][RB + r, PADX:PADX + BS, :] = it[pl.ds(r * BS, BS), :].astype(jnp.bfloat16)
        for c in halo(0):
            c.start()

    phase(
        lambda t: init2[t], stage, recv2, send2, zr2, zs2, xp2, xm2, xf2, xr2, xs2, begin,
    )

    @pl.loop(0, T)
    def _(p):
        t = cls[5, p]
        rowt[p, 0:HALF, :] = lax.select(cls[3, t] == 1, init2[t], recv2[cls[2, t]])
        rowt[p, HALF:, :] = of_four(cls[1, t], stage[t], xp2[t], xf2[t], xm2[t])

    for s in range(ITERS):
        b = pads[s]
        for c in halo(s):
            c.wait()

        @pl.when(g == 0)
        def _():
            b[0:RB, PADX:PADX + BS, :] = jnp.zeros((RB, BS, 128), jnp.bfloat16)

        @pl.when(g == slabs - 1)
        def _():
            b[2 * RB:, PADX:PADX + BS, :] = jnp.zeros((RB, BS, 128), jnp.bfloat16)

        for r in range(RB):
            even = odd = jnp.zeros((TRI, 128), jnp.float32)
            for k in range(NK):
                e, o = product(rowt[r * NK + k], b[col[r, k]])
                even, odd = even + e, odd + o
            spread(mix, r, even, odd)
        for r in range(RB):
            rounded = b[RB + r, PADX:PADX + BS, :].astype(jnp.float32)
            applied = rounded + mix[pl.ds(r * BS, BS), :]
            vec[r, PADX:PADX + BS, :] = (rhs[r].astype(jnp.float32) - applied).astype(jnp.bfloat16)
        for r in range(RB):
            even, odd = product(fac[r], vec[r])
            spread(mix, r, even, odd)
        if s < ITERS - 1:
            for r in range(RB):
                new = it[pl.ds(r * BS, BS), :] + mix[pl.ds(r * BS, BS), :]
                it[pl.ds(r * BS, BS), :] = new
                pads[s + 1][RB + r, PADX:PADX + BS, :] = new.astype(jnp.bfloat16)
            for c in halo(s + 1):
                c.start()
        else:
            for r in range(RB):
                out[r] = it[pl.ds(r * BS, BS), :] + mix[pl.ds(r * BS, BS), :]


def shards(elem_tiles, inv_factor, rhs, mig_source, tile_target, col_index):
    R = 16
    n_pos = 2 * LANES * R
    smem = pl.BlockSpec(memory_space=pltpu.SMEM)
    vmem = pl.BlockSpec(memory_space=pltpu.VMEM)
    bf, f32, i32 = jnp.bfloat16, jnp.float32, jnp.int32
    route, cls, tiles, own, moved = pl.pallas_call(
        functools.partial(prep_kernel, R),
        name="prep",
        out_shape=(
            jax.ShapeDtypeStruct((3, n_pos), i32),
            jax.ShapeDtypeStruct((7, T), i32),
            jax.ShapeDtypeStruct((T, ROWS, 128), bf),
            jax.ShapeDtypeStruct((RB, ROWS, 128), bf),
            jax.ShapeDtypeStruct((2, ROWS, 128), bf),
        ),
        in_specs=[smem, smem, vmem, vmem],
        out_specs=(smem, smem, vmem, vmem, vmem),
        scratch_shapes=[
            pltpu.VMEM((T * ROWS, 128), f32),
            pltpu.VMEM((RB * ROWS, 128), f32),
            pltpu.SMEM((T,), i32),
            pltpu.SMEM((T,), i32),
            pltpu.SMEM((NZ,), i32),
            pltpu.SMEM((T,), i32),
            pltpu.SMEM((T,), i32),
        ],
        compiler_params=pltpu.CompilerParams(vmem_limit_bytes=VMEM_LIMIT),
    )(tile_target, mig_source, elem_tiles, inv_factor)

    half = lambda n: pltpu.VMEM((n, HALF, 128), bf)
    padded = lambda n: pltpu.VMEM((n, 2 * PADX + BS, 128), bf)
    dma = pltpu.SemaphoreType.DMA
    return pl.pallas_call(
        functools.partial(main_kernel, R),
        name="main",
        out_shape=jax.ShapeDtypeStruct((RB, BS, 128), f32),
        in_specs=[smem, smem, smem, vmem, vmem, vmem, vmem],
        out_specs=vmem,
        scratch_shapes=[
            half(n_pos), half(n_pos), half(4 * LANES), half(4 * LANES), half(2 * LANES),
            half(T), half(T), half(T), half(T), half(T), half(T), half(T), half(T),
            pltpu.VMEM((T, ROWS, 128), bf),
            pltpu.VMEM((2, ROWS, 128), bf),
            pltpu.VMEM((RB, ROWS, 128), bf),
            padded(3 * RB), padded(3 * RB), padded(3 * RB), padded(RB),
            pltpu.VMEM((RB * BS, 128), f32),
            pltpu.VMEM((RB * BS, 128), f32),
            dma((n_pos,)), dma((n_pos,)), dma((4 * LANES,)), dma((4 * LANES,)),
            dma((3 * T,)), dma((3 * T,)), dma((3 * T,)), dma((3 * T,)),
            dma((2,)), dma((2,)), dma((2 * ITERS,)), dma((2 * ITERS,)),
        ],
        compiler_params=pltpu.CompilerParams(
            collective_id=0, has_side_effects=True, vmem_limit_bytes=VMEM_LIMIT
        ),
    )(route, cls, col_index, tiles, own, moved, rhs)


def solution(mesh):
    placed = (
        P(("gx", "yz"), None),
        P(("gx", "yz"), None),
        P(("gx", "yz"), None, None),
        P("gx", None),
        P("gx", None),
        P(("gx", "yz"), None),
    )
    return jax.shard_map(
        shards, mesh=mesh, in_specs=placed, out_specs=P(("gx", "yz"), None, None), check_vma=False
    )
```

```python
import functools

import jax
import jax.numpy as jnp
from jax import lax
from jax.experimental import pallas as pl
from jax.experimental.pallas import tpu as pltpu
from jax.sharding import PartitionSpec as P

MESH = pl.DeviceIdType.MESH
ITERS = 3
NX, NZ = 4, 16
NO = NX * NZ
T = 16
RB = 2
NK = 8
BS = 192
ROWS = BS * BS // 128
HALF = ROWS // 2
TRI = BS // 2
LANES = 4
PADX = 64
VMEM_LIMIT = 64_000_000
ROUNDS = (9, 10, 11, 12, 16)
STRIDE = ROWS + 8


def plan_kernel(tmap, mig, route, cls, final, need, sz, srt, cnt):
    my = lax.axis_index("yz")
    z = lax.rem(my, NZ)

    for n, bit in enumerate((NO // 2, 1)):
        q = jnp.bitwise_xor(my, bit)
        b = jnp.int32(0)
        for r in range(RB):
            src = mig[0, q * RB + r]
            b = jnp.where(src // RB == my, lax.rem(src, RB), b)
        cls[6, RB + n] = b
    for r in range(RB):
        src = mig[0, my * RB + r]
        home = src // RB
        cls[6, r] = jnp.where(
            home == my, lax.rem(src, RB), jnp.where(home == jnp.bitwise_xor(my, NO // 2), 2, 3)
        )

    @pl.loop(0, NZ)
    def _(v):
        cnt[v] = 0

    @pl.loop(0, T)
    def _(t):
        s = tmap[0, t] // T
        along = lax.rem(s, NZ)
        sz[t] = along
        cnt[along] = cnt[along] + 1
        across = s // NZ
        cls[0, t] = lax.rem(across + jnp.where(z + along >= NZ, 1, 0), NX)
        cls[1, t] = lax.rem(across + jnp.where(z < along, 1, 0), NX)
        a = lax.rem(my - s + NO, NO)
        cls[5, lax.rem(tmap[0, a * T + t], T)] = t

    def prefix(v, run):
        n = cnt[v]
        cnt[v] = run
        return run + n

    lax.fori_loop(0, NZ, prefix, jnp.int32(0))

    def place(t, far):
        v = sz[t]
        srt[cnt[v]] = t
        cnt[v] = cnt[v] + 1
        return far + NZ - v

    far = lax.fori_loop(0, T, place, jnp.int32(0))

    def split(i, c):
        up, down, best, m = c
        v = sz[srt[i]]
        up, down = up + v, down - (NZ - v)
        worst = jnp.maximum(up, down)
        better = worst < best
        return up, down, jnp.where(better, worst, best), jnp.where(better, i + 1, m)

    zero = jnp.int32(0)
    _, _, most, m = lax.fori_loop(0, T, split, (zero, far, far, zero))
    least = jnp.maximum((most + LANES - 1) // LANES, sz[srt[jnp.maximum(m - 1, 0)]])
    least = jnp.maximum(least, jnp.where(m < T, NZ - sz[srt[jnp.minimum(m, T - 1)]], 0))
    level = zero
    for R in ROUNDS[:-1]:
        level = level + jnp.where(least > R, 1, 0)
    need[...] = jnp.full(need.shape, level, jnp.int32)

    @pl.loop(0, 2 * LANES * ROUNDS[-1])
    def _(p):
        for v in range(len(ROUNDS)):
            route[v, 0, p] = 0
            route[v, 1, p] = 0
            route[v, 2, p] = 0

    def plan(i, ends):
        up, down = ends
        t = srt[i]
        v = sz[t]
        goes_up = i < m
        d = jnp.where(goes_up, v, NZ - v)
        c = jnp.where(goes_up, up, down)
        last = c + d - 1
        cls[3, t] = jnp.where(d == 0, 1, 0)

        for n, R in enumerate(ROUNDS):

            @pl.when((d > 0) & (level <= n))
            def _():
                base = jnp.where(goes_up, 0, LANES * R)
                lane0, lane1 = c // R, last // R

                @pl.when(lane0 == lane1)
                def _():
                    route[n, 0, base + c] = 1
                    route[n, 1, base + c] = t
                    final[n, t] = base + last

                @pl.when(lane0 != lane1)
                def _():
                    route[n, 0, base + lane1 * R] = 1
                    route[n, 1, base + lane1 * R] = t
                    route[n, 0, base + c] = 2
                    route[n, 2, base + last] = 1
                    final[n, t] = base + lane1 * R - 1

        return up + jnp.where(goes_up, d, 0), down + jnp.where(goes_up, 0, d)

    @pl.loop(0, T)
    def _(t):
        for n in range(len(ROUNDS)):
            final[n, t] = 0

    lax.fori_loop(0, T, plan, (zero, zero))


def layout_kernel(cls, need, elem, inv, tiles, own, moved, level, wide, wide2, heard, ss, rs):
    g = lax.axis_index("gx")
    slabs = lax.axis_size("gx")

    def to(k):
        return {"gx": lax.rem(g + k, slabs)}

    def tell(k):
        return pltpu.make_async_remote_copy(
            src_ref=need, dst_ref=heard.at[k], send_sem=ss.at[k], recv_sem=rs.at[k],
            device_id=to(k), device_id_type=MESH,
        )

    barrier = pltpu.get_barrier_semaphore()
    for k in range(1, slabs):
        pl.semaphore_signal(barrier, inc=1, device_id=to(k), device_id_type=MESH)
    pl.semaphore_wait(barrier, slabs - 1)
    for k in range(1, slabs):
        tell(k).start()

    @pl.loop(0, TRI)
    def _(j):
        for k in range(3):
            at = pl.ds(pl.multiple_of((3 * j + k) * 128, 128), 128)
            wide[pl.ds(k * TRI + j, T, stride=STRIDE), :] = elem[:, at].astype(jnp.float32)
            wide2[pl.ds(k * TRI + j, RB, stride=STRIDE), :] = inv[:, at].astype(jnp.float32)

    @pl.loop(0, T)
    def _(t):
        tiles[t] = wide[pl.ds(pl.multiple_of(t * STRIDE, 8), ROWS), :].astype(jnp.bfloat16)

    for b in range(RB):
        own[b] = wide2[pl.ds(b * STRIDE, ROWS), :].astype(jnp.bfloat16)
    for n in range(2):
        moved[n] = own[cls[6, RB + n]]

    most = need[...]
    for k in range(1, slabs):
        tell(k).wait()
        most = jnp.maximum(most, heard[k])
    level[...] = most


def main_kernel(
    v, route, cls, final, col, tiles, own, moved, rhs, out,
    recv1, recv2, send1, send2, save, xp1, xm1, xf1, xp2, xm2, xf2, init2, stage, rowt,
    got, fac, pad0, pad1, pad2, vec, mix, it,
    zr1, zr2, zs1, zs2, xr1, xr2, xs1, xs2, mr, ms, hr, hs,
):
    R = ROUNDS[v]
    g = lax.axis_index("gx")
    slabs = lax.axis_size("gx")
    my = lax.axis_index("yz")
    x, z = my // NZ, lax.rem(my, NZ)
    line = x * NZ
    z_to = ({"yz": line + lax.rem(z + 1, NZ)}, {"yz": line + lax.rem(z + NZ - 1, NZ)})
    x_to = ({"yz": lax.rem(x + 1, NX) * NZ + z}, {"yz": lax.rem(x + NX - 1, NX) * NZ + z})
    m_to = ({"yz": lax.rem(x + NX // 2, NX) * NZ + z}, {"yz": my + 1 - 2 * lax.rem(my, 2)})
    g_to = ({"gx": lax.rem(g + 1, slabs)}, {"gx": lax.rem(g + slabs - 1, slabs)})
    pads = (pad0, pad1, pad2)

    def remote(src, dst, send, recv, to):
        return pltpu.make_async_remote_copy(
            src_ref=src, dst_ref=dst, send_sem=send, recv_sem=recv, device_id=to, device_id_type=MESH
        )

    barrier = pltpu.get_barrier_semaphore()
    greet = (*z_to, *x_to, m_to[0], *g_to)
    for to in greet:
        pl.semaphore_signal(barrier, inc=1, device_id=to, device_id_type=MESH)
    pl.semaphore_wait(barrier, len(greet))

    def moves():
        return [remote(moved.at[n], got.at[n], ms.at[n], mr.at[n], m_to[n]) for n in range(2)]

    for c in moves():
        c.start()

    for buf in (*pads, vec):
        n = buf.shape[0]
        buf[:, 0:PADX, :] = jnp.zeros((n, PADX, 128), jnp.bfloat16)
        buf[:, PADX + BS:, :] = jnp.zeros((n, PADX, 128), jnp.bfloat16)
    save[...] = jnp.zeros_like(save)

    lanes = [(d, j) for j in reversed(range(LANES)) for d in range(2)]

    def z_copy(recv, sendb, zr, zs, d, j, r):
        p = (d * LANES + j) * R + r
        k = (d * LANES + j) * 2 + lax.rem(r, 2)
        return remote(sendb.at[k], recv.at[p], zs.at[k], zr.at[p], z_to[d])

    def x_first(src, xp, xm, xr, xs, t, d):
        return remote(src.at[t], (xp, xm)[d].at[t], xs.at[d * T + t], xr.at[d * T + t], x_to[d])

    def x_second(xp, xm, xf, xr, xs, t, odd):
        src = (xm if odd else xp).at[t]
        return remote(src, xf.at[t], xs.at[2 * T + t], xr.at[2 * T + t], x_to[1 if odd else 0])

    def phase(first, x_src, recv, sendb, zr, zs, xp, xm, xf, xr, xs, between):
        pend = None
        for d, j in lanes:
            k = (d * LANES + j) * 2
            sendb[k] = first(route[v, 1, (d * LANES + j) * R])
            if pend is not None:
                pend.start()
            pend = z_copy(recv, sendb, zr, zs, d, j, 0)
        pend.start()

        @pl.loop(0, T)
        def _(t):
            for d in range(2):
                x_first(x_src, xp, xm, xr, xs, t, d).start()

        if between is not None:
            between()

        @pl.loop(1, R)
        def _(r):
            for d, j in lanes:
                p = (d * LANES + j) * R + r
                z_copy(recv, sendb, zr, zs, d, j, r - 1).wait_recv()
                come = recv[p - 1]
                mode = route[v, 0, p]
                new = first(route[v, 1, p])
                if j < LANES - 1:
                    new = lax.select(mode == 2, save[d * LANES + j + 1], new)
                new = lax.select(mode == 0, come, new)

                @pl.when(r >= 2)
                def _():
                    z_copy(recv, sendb, zr, zs, d, j, r - 2).wait_send()

                sendb[(d * LANES + j) * 2 + lax.rem(r, 2)] = new
                if j > 0:
                    s = d * LANES + j
                    save[s] = lax.select(route[v, 2, p - 1] == 1, come, save[s])
                z_copy(recv, sendb, zr, zs, d, j, r).start()

            @pl.when(r <= T // 2)
            def _():
                t = 2 * (r - 1)
                x_first(x_src, xp, xm, xr, xs, t, 0).wait_recv()
                x_second(xp, xm, xf, xr, xs, t, False).start()
                x_first(x_src, xp, xm, xr, xs, t + 1, 1).wait_recv()
                x_second(xp, xm, xf, xr, xs, t + 1, True).start()

        @pl.loop(0, T // 2)
        def _(h):
            t = 2 * h
            x_first(x_src, xp, xm, xr, xs, t, 0).wait_send()
            x_first(x_src, xp, xm, xr, xs, t, 1).wait()
            x_first(x_src, xp, xm, xr, xs, t + 1, 0).wait()
            x_first(x_src, xp, xm, xr, xs, t + 1, 1).wait_send()
            for c in (x_second(xp, xm, xf, xr, xs, t, False), x_second(xp, xm, xf, xr, xs, t + 1, True)):
                c.wait()

        for d, j in lanes:
            last = z_copy(recv, sendb, zr, zs, d, j, R - 1)
            last.wait()
            z_copy(recv, sendb, zr, zs, d, j, R - 2).wait_send()

    def of_four(n, a, b, c, d):
        return lax.select(n == 0, a, lax.select(n == 1, b, lax.select(n == 2, c, d)))

    phase(
        lambda t: tiles[t, HALF:, :], tiles.at[:, 0:HALF, :], recv1, send1, zr1, zs1,
        xp1, xm1, xf1, xr1, xs1, None,
    )

    @pl.loop(0, T)
    def _(t):
        stage[t] = lax.select(cls[3, t] == 1, tiles[t, HALF:, :], recv1[final[v, t]])
        init2[t] = of_four(cls[0, t], tiles[t, 0:HALF, :], xp1[t], xf1[t], xm1[t])

    def product(m, v):
        f0, f1, f2 = m[0:TRI], m[TRI:2 * TRI], m[2 * TRI:]
        even = jnp.dot(
            jnp.concatenate([f0, f1], axis=1), v[PADX:, :], preferred_element_type=jnp.float32
        )
        odd = jnp.dot(
            jnp.concatenate([f1, f2], axis=1), v[:PADX + BS, :], preferred_element_type=jnp.float32
        )
        return even, odd

    def halo(s):
        b = pads[s]
        mine = b.at[RB:2 * RB, PADX:PADX + BS, :]
        return (
            remote(mine, b.at[0:RB, PADX:PADX + BS, :], hs.at[2 * s], hr.at[2 * s], g_to[0]),
            remote(mine, b.at[2 * RB:, PADX:PADX + BS, :], hs.at[2 * s + 1], hr.at[2 * s + 1], g_to[1]),
        )

    def spread(ref, r, even, odd):
        ref[pl.ds(r * BS, TRI, stride=2), :] = even
        ref[pl.ds(r * BS + 1, TRI, stride=2), :] = odd

    def begin():
        for c in moves():
            c.wait()
        for r in range(RB):
            fac[r] = of_four(cls[6, r], own[0], own[1], got[0], got[1])
            vec[r, PADX:PADX + BS, :] = rhs[r]
        for r in range(RB):
            even, odd = product(fac[r], vec[r])
            spread(it, r, even, odd)
        for r in range(RB):
            pads[0][RB + r, PADX:PADX + BS, :] = it[pl.ds(r * BS, BS), :].astype(jnp.bfloat16)
        for c in halo(0):
            c.start()

    phase(
        lambda t: init2[t], stage, recv2, send2, zr2, zs2, xp2, xm2, xf2, xr2, xs2, begin,
    )

    @pl.loop(0, T)
    def _(p):
        t = cls[5, p]
        rowt[p, 0:HALF, :] = lax.select(cls[3, t] == 1, init2[t], recv2[final[v, t]])
        rowt[p, HALF:, :] = of_four(cls[1, t], stage[t], xp2[t], xf2[t], xm2[t])

    for s in range(ITERS):
        b = pads[s]
        for c in halo(s):
            c.wait()

        @pl.when(g == 0)
        def _():
            b[0:RB, PADX:PADX + BS, :] = jnp.zeros((RB, BS, 128), jnp.bfloat16)

        @pl.when(g == slabs - 1)
        def _():
            b[2 * RB:, PADX:PADX + BS, :] = jnp.zeros((RB, BS, 128), jnp.bfloat16)

        for r in range(RB):
            even = odd = jnp.zeros((TRI, 128), jnp.float32)
            for k in range(NK):
                e, o = product(rowt[r * NK + k], b[col[r, k]])
                even, odd = even + e, odd + o
            spread(mix, r, even, odd)
        for r in range(RB):
            rounded = b[RB + r, PADX:PADX + BS, :].astype(jnp.float32)
            applied = rounded + mix[pl.ds(r * BS, BS), :]
            vec[r, PADX:PADX + BS, :] = (rhs[r].astype(jnp.float32) - applied).astype(jnp.bfloat16)
        for r in range(RB):
            even, odd = product(fac[r], vec[r])
            spread(mix, r, even, odd)
        if s < ITERS - 1:
            for r in range(RB):
                new = it[pl.ds(r * BS, BS), :] + mix[pl.ds(r * BS, BS), :]
                it[pl.ds(r * BS, BS), :] = new
                pads[s + 1][RB + r, PADX:PADX + BS, :] = new.astype(jnp.bfloat16)
            for c in halo(s + 1):
                c.start()
        else:
            for r in range(RB):
                out[r] = it[pl.ds(r * BS, BS), :] + mix[pl.ds(r * BS, BS), :]


def call_main(v, route, cls, final, col, tiles, own, moved, rhs):
    n_pos = 2 * LANES * ROUNDS[v]
    smem = pl.BlockSpec(memory_space=pltpu.SMEM)
    vmem = pl.BlockSpec(memory_space=pltpu.VMEM)
    bf, f32 = jnp.bfloat16, jnp.float32
    half = lambda n: pltpu.VMEM((n, HALF, 128), bf)
    padded = lambda n: pltpu.VMEM((n, 2 * PADX + BS, 128), bf)
    dma = pltpu.SemaphoreType.DMA
    return pl.pallas_call(
        functools.partial(main_kernel, v),
        name="main%d" % ROUNDS[v],
        out_shape=jax.ShapeDtypeStruct((RB, BS, 128), f32),
        in_specs=[smem, smem, smem, smem, vmem, vmem, vmem, vmem],
        out_specs=vmem,
        scratch_shapes=[
            half(n_pos), half(n_pos), half(4 * LANES), half(4 * LANES), half(2 * LANES),
            half(T), half(T), half(T), half(T), half(T), half(T), half(T), half(T),
            pltpu.VMEM((T, ROWS, 128), bf),
            pltpu.VMEM((2, ROWS, 128), bf),
            pltpu.VMEM((RB, ROWS, 128), bf),
            padded(3 * RB), padded(3 * RB), padded(3 * RB), padded(RB),
            pltpu.VMEM((RB * BS, 128), f32),
            pltpu.VMEM((RB * BS, 128), f32),
            dma((n_pos,)), dma((n_pos,)), dma((4 * LANES,)), dma((4 * LANES,)),
            dma((3 * T,)), dma((3 * T,)), dma((3 * T,)), dma((3 * T,)),
            dma((2,)), dma((2,)), dma((2 * ITERS,)), dma((2 * ITERS,)),
        ],
        compiler_params=pltpu.CompilerParams(
            collective_id=1 + v, has_side_effects=True, vmem_limit_bytes=VMEM_LIMIT
        ),
    )(route, cls, final, col, tiles, own, moved, rhs)


def shards(elem_tiles, inv_factor, rhs, mig_source, tile_target, col_index):
    smem = pl.BlockSpec(memory_space=pltpu.SMEM)
    vmem = pl.BlockSpec(memory_space=pltpu.VMEM)
    bf, f32, i32 = jnp.bfloat16, jnp.float32, jnp.int32
    slabs = lax.axis_size("gx")
    route, cls, final, need = pl.pallas_call(
        plan_kernel,
        name="plan",
        out_shape=(
            jax.ShapeDtypeStruct((len(ROUNDS), 3, 2 * LANES * ROUNDS[-1]), i32),
            jax.ShapeDtypeStruct((7, T), i32),
            jax.ShapeDtypeStruct((len(ROUNDS), T), i32),
            jax.ShapeDtypeStruct((8, 128), i32),
        ),
        in_specs=[smem, smem],
        out_specs=(smem, smem, smem, vmem),
        scratch_shapes=[pltpu.SMEM((T,), i32), pltpu.SMEM((T,), i32), pltpu.SMEM((NZ,), i32)],
    )(tile_target, mig_source)

    tiles, own, moved, level = pl.pallas_call(
        layout_kernel,
        name="layout",
        out_shape=(
            jax.ShapeDtypeStruct((T, ROWS, 128), bf),
            jax.ShapeDtypeStruct((RB, ROWS, 128), bf),
            jax.ShapeDtypeStruct((2, ROWS, 128), bf),
            jax.ShapeDtypeStruct((8, 128), i32),
        ),
        in_specs=[smem, vmem, vmem, vmem],
        out_specs=(vmem, vmem, vmem, vmem),
        scratch_shapes=[
            pltpu.VMEM((T * STRIDE, 128), f32),
            pltpu.VMEM((RB * STRIDE, 128), f32),
            pltpu.VMEM((slabs, 8, 128), i32),
            pltpu.SemaphoreType.DMA((slabs,)),
            pltpu.SemaphoreType.DMA((slabs,)),
        ],
        compiler_params=pltpu.CompilerParams(
            collective_id=0, has_side_effects=True, vmem_limit_bytes=VMEM_LIMIT
        ),
    )(cls, need, elem_tiles, inv_factor)

    return lax.switch(
        level[0, 0],
        [functools.partial(call_main, v) for v in range(len(ROUNDS))],
        route, cls, final, col_index, tiles, own, moved, rhs,
    )


def solution(mesh):
    placed = (
        P(("gx", "yz"), None),
        P(("gx", "yz"), None),
        P(("gx", "yz"), None, None),
        P("gx", None),
        P("gx", None),
        P(("gx", "yz"), None),
    )
    return jax.shard_map(
        shards, mesh=mesh, in_specs=placed, out_specs=P(("gx", "yz"), None, None), check_vma=False
    )
```

```python
import functools

import jax
import jax.numpy as jnp
from jax import lax
from jax.experimental import pallas as pl
from jax.experimental.pallas import tpu as pltpu
from jax.sharding import PartitionSpec as P

MESH = pl.DeviceIdType.MESH
ITERS = 3
NX, NZ = 4, 16
NO = NX * NZ
T = 16
RB = 2
NK = 8
BS = 192
ROWS = BS * BS // 128
HALF = ROWS // 2
TRI = BS // 2
LANES = 4
PADX = 64
VMEM_LIMIT = 64_000_000
ROUNDS = (9, 10, 11, 16)
STRIDE = ROWS + 8


def sort_up(values):
    v, n, p = list(values), len(values), 1
    while p < n:
        k = p
        while k >= 1:
            for j in range(k % p, n - k, 2 * k):
                for i in range(j, j + min(k, n - j - k)):
                    if i // (2 * p) == (i + k) // (2 * p):
                        v[i], v[i + k] = jnp.minimum(v[i], v[i + k]), jnp.maximum(v[i], v[i + k])
            k //= 2
        p *= 2
    return v


def prep_kernel(
    tmap, mig, elem, inv, tiles, own, moved, route, place, cls, final, level,
    need, wide, wide2, heard, ss, rs,
):
    g = lax.axis_index("gx")
    slabs = lax.axis_size("gx")
    my = lax.axis_index("yz")
    z = my & (NZ - 1)

    def to(k):
        return {"gx": lax.rem(g + k, slabs)}

    def tell(k):
        return pltpu.make_async_remote_copy(
            src_ref=need, dst_ref=heard.at[k], send_sem=ss.at[k], recv_sem=rs.at[k],
            device_id=to(k), device_id_type=MESH,
        )

    barrier = pltpu.get_barrier_semaphore()
    for k in range(1, slabs):
        pl.semaphore_signal(barrier, inc=1, device_id=to(k), device_id_type=MESH)

    shift = [tmap[0, t] >> 4 for t in range(T)]
    along = [s & (NZ - 1) for s in shift]
    up = m = jnp.int32(0)
    down = most = sum(NZ - a for a in along)
    near = sort_up(along)
    for i, v in enumerate(near):
        up, down = up + v, down + v - NZ
        worst = jnp.maximum(up, down)
        m = jnp.where(worst < most, i + 1, m)
        most = jnp.minimum(most, worst)
    least = (most + LANES - 1) >> 2
    for i, v in enumerate(near):
        least = jnp.maximum(least, jnp.where(i < m, v, NZ - v))
    mine = jnp.int32(0)
    for R in ROUNDS[:-1]:
        mine = mine + jnp.where(least > R, 1, 0)
    need[...] = jnp.full(need.shape, mine, jnp.int32)

    @pl.loop(0, TRI)
    def _(j):
        for k in range(3):
            at = pl.ds(pl.multiple_of((3 * j + k) * 128, 128), 128)
            wide[pl.ds(k * TRI + j, T, stride=STRIDE), :] = elem[:, at].astype(jnp.float32)
            wide2[pl.ds(k * TRI + j, RB, stride=STRIDE), :] = inv[:, at].astype(jnp.float32)

    pl.semaphore_wait(barrier, slabs - 1)
    for k in range(1, slabs):
        tell(k).start()

    leaving = []
    for bit in (NO // 2, 1):
        q = my ^ bit
        b = jnp.int32(0)
        for r in range(RB):
            src = mig[0, q * RB + r]
            b = jnp.where(src >> 1 == my, src & 1, b)
        leaving.append(b)
    for r in range(RB):
        src = mig[0, my * RB + r]
        home = src >> 1
        cls[3, r] = jnp.where(home == my, src & 1, jnp.where(home == my ^ (NO // 2), 2, 3))

    lane = lax.broadcasted_iota(jnp.int32, (1, 128), 1)
    rank = [jnp.int32(0)] * T
    fills = jnp.zeros((1, 128), jnp.int32)
    for t in range(T):
        across = shift[t] >> 4
        cls[0, t] = (across + ((z + along[t]) >> 4)) & (NX - 1)
        cls[1, t] = (across + (((z - along[t]) >> 31) & 1)) & (NX - 1)
        a = (my - shift[t]) & (NO - 1)
        fills = jnp.where(lane == (tmap[0, a * T + t] & (T - 1)), t, fills)
        for u in range(t):
            before = ((along[t] - along[u]) >> 31) & 1
            rank[u] = rank[u] + before
            rank[t] = rank[t] + 1 - before
    place[...] = fills

    goes_up = [rank[t] < m for t in range(T)]
    dist = [jnp.where(goes_up[t], along[t], NZ - along[t]) for t in range(T)]
    at_up = at_down = jnp.int32(0)
    start = []
    for t in range(T):
        start.append(jnp.where(goes_up[t], at_up, at_down))
        at_up = at_up + jnp.where(goes_up[t], dist[t], 0)
        at_down = at_down + jnp.where(goes_up[t], 0, dist[t])
        cls[2, t] = jnp.where(dist[t] == 0, 1, 0)

    for n, R in enumerate(ROUNDS):
        magic = 65536 // R + 1
        entry = jnp.zeros((1, 128), jnp.int32)
        for t in range(T):
            c, d = start[t], dist[t]
            base = jnp.where(goes_up[t], 0, LANES * R)
            last = c + d - 1
            lane1 = (last * magic) >> 16
            wraps = lane1 * R > c
            head = jnp.where(wraps, lane1 * R, c)
            moves = d > 0
            wraps = wraps & moves
            entry = jnp.where(lane == jnp.where(moves, base + head, -1), 1 + 4 * t, entry)
            entry = jnp.where(lane == jnp.where(wraps, base + c, -1), 2, entry)
            entry = jnp.where(lane == jnp.where(wraps, base + last, -1), entry + 256, entry)
            final[n, t] = jnp.where(
                moves, jnp.maximum(base + jnp.where(wraps, head - 1, last), 0), 0
            )
        route[n:n + 1, :] = entry

    @pl.loop(0, T)
    def _(t):
        tiles[t] = wide[pl.ds(pl.multiple_of(t * STRIDE, 8), ROWS), :].astype(jnp.bfloat16)

    for b in range(RB):
        own[b] = wide2[pl.ds(b * STRIDE, ROWS), :].astype(jnp.bfloat16)
    for n in range(2):
        moved[n] = own[leaving[n]]

    top = need[...]
    for k in range(1, slabs):
        tell(k).wait()
        top = jnp.maximum(top, heard[k])
    level[0, 0] = jnp.max(top)


def main_kernel(
    v, route, place, cls, final, col, tiles, own, moved, rhs, out,
    recv1, recv2, send1, send2, save, xp1, xm1, xf1, xp2, xm2, xf2, init2, stage, rowt,
    got, fac, pad0, pad1, pad2, vec, mix, it,
    zr1, zr2, zs1, zs2, xr1, xr2, xs1, xs2, mr, ms, hr, hs,
):
    R = ROUNDS[v]
    g = lax.axis_index("gx")
    slabs = lax.axis_size("gx")
    my = lax.axis_index("yz")
    x, z = my // NZ, lax.rem(my, NZ)
    line = x * NZ
    z_to = ({"yz": line + lax.rem(z + 1, NZ)}, {"yz": line + lax.rem(z + NZ - 1, NZ)})
    x_to = ({"yz": lax.rem(x + 1, NX) * NZ + z}, {"yz": lax.rem(x + NX - 1, NX) * NZ + z})
    m_to = ({"yz": lax.rem(x + NX // 2, NX) * NZ + z}, {"yz": my + 1 - 2 * lax.rem(my, 2)})
    g_to = ({"gx": lax.rem(g + 1, slabs)}, {"gx": lax.rem(g + slabs - 1, slabs)})
    pads = (pad0, pad1, pad2)

    def remote(src, dst, send, recv, to):
        return pltpu.make_async_remote_copy(
            src_ref=src, dst_ref=dst, send_sem=send, recv_sem=recv, device_id=to, device_id_type=MESH
        )

    barrier = pltpu.get_barrier_semaphore()
    greet = (*z_to, *x_to, m_to[0], *g_to)
    for to in greet:
        pl.semaphore_signal(barrier, inc=1, device_id=to, device_id_type=MESH)

    def moves():
        return [remote(moved.at[n], got.at[n], ms.at[n], mr.at[n], m_to[n]) for n in range(2)]

    for buf in (*pads, vec):
        n = buf.shape[0]
        buf[:, 0:PADX, :] = jnp.zeros((n, PADX, 128), jnp.bfloat16)
        buf[:, PADX + BS:, :] = jnp.zeros((n, PADX, 128), jnp.bfloat16)
    save[...] = jnp.zeros_like(save)
    pl.semaphore_wait(barrier, len(greet))
    for c in moves():
        c.start()

    lanes = [(d, j) for j in reversed(range(LANES)) for d in range(2)]

    def z_copy(recv, sendb, zr, zs, d, j, r):
        p = (d * LANES + j) * R + r
        k = (d * LANES + j) * 2 + (r & 1)
        return remote(sendb.at[k], recv.at[p], zs.at[k], zr.at[p], z_to[d])

    def x_first(src, xp, xm, xr, xs, t, d):
        return remote(src.at[t], (xp, xm)[d].at[t], xs.at[d * T + t], xr.at[d * T + t], x_to[d])

    def x_second(xp, xm, xf, xr, xs, t, odd):
        src = (xm if odd else xp).at[t]
        return remote(src, xf.at[t], xs.at[2 * T + t], xr.at[2 * T + t], x_to[1 if odd else 0])

    def phase(first, x_src, recv, sendb, zr, zs, xp, xm, xf, xr, xs, between):
        pend = None
        for d, j in lanes:
            k = (d * LANES + j) * 2
            sendb[k] = first(route[v, (d * LANES + j) * R] >> 2 & (T - 1))
            if pend is not None:
                pend.start()
            pend = z_copy(recv, sendb, zr, zs, d, j, 0)
        pend.start()

        @pl.loop(0, T)
        def _(t):
            for d in range(2):
                x_first(x_src, xp, xm, xr, xs, t, d).start()

        if between is not None:
            between()

        @pl.loop(1, R)
        def _(r):
            for d, j in lanes:
                p = (d * LANES + j) * R + r
                z_copy(recv, sendb, zr, zs, d, j, r - 1).wait_recv()
                come = recv[p - 1]
                mode = route[v, p] & 3
                new = first(route[v, p] >> 2 & (T - 1))
                if j < LANES - 1:
                    new = lax.select(mode == 2, save[d * LANES + j + 1], new)
                new = lax.select(mode == 0, come, new)

                @pl.when(r >= 2)
                def _():
                    z_copy(recv, sendb, zr, zs, d, j, r - 2).wait_send()

                sendb[(d * LANES + j) * 2 + (r & 1)] = new
                if j > 0:
                    s = d * LANES + j
                    save[s] = lax.select(route[v, p - 1] >= 256, come, save[s])
                z_copy(recv, sendb, zr, zs, d, j, r).start()

            @pl.when(r <= T // 2)
            def _():
                t = 2 * (r - 1)
                x_first(x_src, xp, xm, xr, xs, t, 0).wait_recv()
                x_second(xp, xm, xf, xr, xs, t, False).start()
                x_first(x_src, xp, xm, xr, xs, t + 1, 1).wait_recv()
                x_second(xp, xm, xf, xr, xs, t + 1, True).start()

        @pl.loop(0, T // 2)
        def _(h):
            t = 2 * h
            x_first(x_src, xp, xm, xr, xs, t, 0).wait_send()
            x_first(x_src, xp, xm, xr, xs, t, 1).wait()
            x_first(x_src, xp, xm, xr, xs, t + 1, 0).wait()
            x_first(x_src, xp, xm, xr, xs, t + 1, 1).wait_send()
            for c in (x_second(xp, xm, xf, xr, xs, t, False), x_second(xp, xm, xf, xr, xs, t + 1, True)):
                c.wait()

        for d, j in lanes:
            last = z_copy(recv, sendb, zr, zs, d, j, R - 1)
            last.wait()
            z_copy(recv, sendb, zr, zs, d, j, R - 2).wait_send()

    def of_four(n, a, b, c, d):
        return lax.select(n == 0, a, lax.select(n == 1, b, lax.select(n == 2, c, d)))

    phase(
        lambda t: tiles[t, HALF:, :], tiles.at[:, 0:HALF, :], recv1, send1, zr1, zs1,
        xp1, xm1, xf1, xr1, xs1, None,
    )

    @pl.loop(0, T)
    def _(t):
        stage[t] = lax.select(cls[2, t] == 1, tiles[t, HALF:, :], recv1[final[v, t]])
        init2[t] = of_four(cls[0, t], tiles[t, 0:HALF, :], xp1[t], xf1[t], xm1[t])

    def product(m, v):
        f0, f1, f2 = m[0:TRI], m[TRI:2 * TRI], m[2 * TRI:]
        even = jnp.dot(
            jnp.concatenate([f0, f1], axis=1), v[PADX:, :], preferred_element_type=jnp.float32
        )
        odd = jnp.dot(
            jnp.concatenate([f1, f2], axis=1), v[:PADX + BS, :], preferred_element_type=jnp.float32
        )
        return even, odd

    def halo(s):
        b = pads[s]
        mine = b.at[RB:2 * RB, PADX:PADX + BS, :]
        return (
            remote(mine, b.at[0:RB, PADX:PADX + BS, :], hs.at[2 * s], hr.at[2 * s], g_to[0]),
            remote(mine, b.at[2 * RB:, PADX:PADX + BS, :], hs.at[2 * s + 1], hr.at[2 * s + 1], g_to[1]),
        )

    def spread(ref, r, even, odd):
        ref[pl.ds(r * BS, TRI, stride=2), :] = even
        ref[pl.ds(r * BS + 1, TRI, stride=2), :] = odd

    def begin():
        for c in moves():
            c.wait()
        for r in range(RB):
            fac[r] = of_four(cls[3, r], own[0], own[1], got[0], got[1])
            vec[r, PADX:PADX + BS, :] = rhs[r]
        for r in range(RB):
            even, odd = product(fac[r], vec[r])
            spread(it, r, even, odd)
        for r in range(RB):
            pads[0][RB + r, PADX:PADX + BS, :] = it[pl.ds(r * BS, BS), :].astype(jnp.bfloat16)
        for c in halo(0):
            c.start()

    phase(
        lambda t: init2[t], stage, recv2, send2, zr2, zs2, xp2, xm2, xf2, xr2, xs2, begin,
    )

    @pl.loop(0, T)
    def _(p):
        t = place[0, p]
        rowt[p, 0:HALF, :] = lax.select(cls[2, t] == 1, init2[t], recv2[final[v, t]])
        rowt[p, HALF:, :] = of_four(cls[1, t], stage[t], xp2[t], xf2[t], xm2[t])

    for s in range(ITERS):
        b = pads[s]
        for c in halo(s):
            c.wait()

        @pl.when(g == 0)
        def _():
            b[0:RB, PADX:PADX + BS, :] = jnp.zeros((RB, BS, 128), jnp.bfloat16)

        @pl.when(g == slabs - 1)
        def _():
            b[2 * RB:, PADX:PADX + BS, :] = jnp.zeros((RB, BS, 128), jnp.bfloat16)

        for r in range(RB):
            even = odd = jnp.zeros((TRI, 128), jnp.float32)
            for k in range(NK):
                e, o = product(rowt[r * NK + k], b[col[r, k]])
                even, odd = even + e, odd + o
            spread(mix, r, even, odd)
        for r in range(RB):
            rounded = b[RB + r, PADX:PADX + BS, :].astype(jnp.float32)
            applied = rounded + mix[pl.ds(r * BS, BS), :]
            vec[r, PADX:PADX + BS, :] = (rhs[r].astype(jnp.float32) - applied).astype(jnp.bfloat16)
        for r in range(RB):
            even, odd = product(fac[r], vec[r])
            spread(mix, r, even, odd)
        if s < ITERS - 1:
            for r in range(RB):
                new = it[pl.ds(r * BS, BS), :] + mix[pl.ds(r * BS, BS), :]
                it[pl.ds(r * BS, BS), :] = new
                pads[s + 1][RB + r, PADX:PADX + BS, :] = new.astype(jnp.bfloat16)
            for c in halo(s + 1):
                c.start()
        else:
            for r in range(RB):
                out[r] = it[pl.ds(r * BS, BS), :] + mix[pl.ds(r * BS, BS), :]


def call_main(v, route, place, cls, final, col, tiles, own, moved, rhs):
    n_pos = 2 * LANES * ROUNDS[v]
    smem = pl.BlockSpec(memory_space=pltpu.SMEM)
    vmem = pl.BlockSpec(memory_space=pltpu.VMEM)
    bf, f32 = jnp.bfloat16, jnp.float32
    half = lambda n: pltpu.VMEM((n, HALF, 128), bf)
    padded = lambda n: pltpu.VMEM((n, 2 * PADX + BS, 128), bf)
    dma = pltpu.SemaphoreType.DMA
    return pl.pallas_call(
        functools.partial(main_kernel, v),
        name="main%d" % ROUNDS[v],
        out_shape=jax.ShapeDtypeStruct((RB, BS, 128), f32),
        in_specs=[smem] * 5 + [vmem] * 4,
        out_specs=vmem,
        scratch_shapes=[
            half(n_pos), half(n_pos), half(4 * LANES), half(4 * LANES), half(2 * LANES),
            half(T), half(T), half(T), half(T), half(T), half(T), half(T), half(T),
            pltpu.VMEM((T, ROWS, 128), bf),
            pltpu.VMEM((2, ROWS, 128), bf),
            pltpu.VMEM((RB, ROWS, 128), bf),
            padded(3 * RB), padded(3 * RB), padded(3 * RB), padded(RB),
            pltpu.VMEM((RB * BS, 128), f32),
            pltpu.VMEM((RB * BS, 128), f32),
            dma((n_pos,)), dma((n_pos,)), dma((4 * LANES,)), dma((4 * LANES,)),
            dma((3 * T,)), dma((3 * T,)), dma((3 * T,)), dma((3 * T,)),
            dma((2,)), dma((2,)), dma((2 * ITERS,)), dma((2 * ITERS,)),
        ],
        compiler_params=pltpu.CompilerParams(
            collective_id=1 + v, has_side_effects=True, vmem_limit_bytes=VMEM_LIMIT
        ),
    )(route, place, cls, final, col, tiles, own, moved, rhs)


def shards(elem_tiles, inv_factor, rhs, mig_source, tile_target, col_index):
    smem = pl.BlockSpec(memory_space=pltpu.SMEM)
    vmem = pl.BlockSpec(memory_space=pltpu.VMEM)
    bf, f32, i32 = jnp.bfloat16, jnp.float32, jnp.int32
    slabs = lax.axis_size("gx")
    rounds = len(ROUNDS)
    tiles, own, moved, route, place, cls, final, level = pl.pallas_call(
        prep_kernel,
        name="prep",
        out_shape=(
            jax.ShapeDtypeStruct((T, ROWS, 128), bf),
            jax.ShapeDtypeStruct((RB, ROWS, 128), bf),
            jax.ShapeDtypeStruct((2, ROWS, 128), bf),
            jax.ShapeDtypeStruct((rounds, 128), i32),
            jax.ShapeDtypeStruct((1, 128), i32),
            jax.ShapeDtypeStruct((4, T), i32),
            jax.ShapeDtypeStruct((rounds, T), i32),
            jax.ShapeDtypeStruct((1, 1), i32),
        ),
        in_specs=[smem, smem, vmem, vmem],
        out_specs=(vmem,) * 5 + (smem,) * 3,
        scratch_shapes=[
            pltpu.VMEM((8, 128), i32),
            pltpu.VMEM((T * STRIDE, 128), f32),
            pltpu.VMEM((RB * STRIDE, 128), f32),
            pltpu.VMEM((slabs, 8, 128), i32),
            pltpu.SemaphoreType.DMA((slabs,)),
            pltpu.SemaphoreType.DMA((slabs,)),
        ],
        compiler_params=pltpu.CompilerParams(
            collective_id=0, has_side_effects=True, vmem_limit_bytes=VMEM_LIMIT
        ),
    )(tile_target, mig_source, elem_tiles, inv_factor)

    return lax.switch(
        level[0, 0],
        [functools.partial(call_main, v) for v in range(len(ROUNDS))],
        route, place, cls, final, col_index, tiles, own, moved, rhs,
    )


def solution(mesh):
    placed = (
        P(("gx", "yz"), None),
        P(("gx", "yz"), None),
        P(("gx", "yz"), None, None),
        P("gx", None),
        P("gx", None),
        P(("gx", "yz"), None),
    )
    return jax.shard_map(
        shards, mesh=mesh, in_specs=placed, out_specs=P(("gx", "yz"), None, None), check_vma=False
    )
```

```python
import functools

import jax
import jax.numpy as jnp
from jax import lax
from jax.experimental import pallas as pl
from jax.experimental.pallas import tpu as pltpu
from jax.sharding import PartitionSpec as P

MESH = pl.DeviceIdType.MESH
ITERS = 3
NX, NZ = 4, 16
NO = NX * NZ
T = 16
RB = 2
NK = 8
BS = 192
ROWS = BS * BS // 128
HALF = ROWS // 2
TRI = BS // 2
LANES = 4
PADX = 64
VMEM_LIMIT = 64_000_000
ROUNDS = (9, 10, 11, 16)
STRIDE = ROWS + 8


def sort_up(values):
    v, n, p = list(values), len(values), 1
    while p < n:
        k = p
        while k >= 1:
            for j in range(k % p, n - k, 2 * k):
                for i in range(j, j + min(k, n - j - k)):
                    if i // (2 * p) == (i + k) // (2 * p):
                        v[i], v[i + k] = jnp.minimum(v[i], v[i + k]), jnp.maximum(v[i], v[i + k])
            k //= 2
        p *= 2
    return v


def prep_kernel(
    tmap, mig, elem, inv, tiles, own, moved, route, place, cls, final, level,
    need, wide, wide2, heard, ss, rs,
):
    g = lax.axis_index("gx")
    slabs = lax.axis_size("gx")
    my = lax.axis_index("yz")
    z = my & (NZ - 1)

    def to(k):
        return {"gx": lax.rem(g + k, slabs)}

    def tell(k):
        return pltpu.make_async_remote_copy(
            src_ref=need, dst_ref=heard.at[k], send_sem=ss.at[k], recv_sem=rs.at[k],
            device_id=to(k), device_id_type=MESH,
        )

    barrier = pltpu.get_barrier_semaphore()
    for k in range(1, slabs):
        pl.semaphore_signal(barrier, inc=1, device_id=to(k), device_id_type=MESH)

    shift = [tmap[0, t] >> 4 for t in range(T)]
    along = [s & (NZ - 1) for s in shift]
    up = m = jnp.int32(0)
    down = most = sum(NZ - a for a in along)
    near = sort_up(along)
    for i, v in enumerate(near):
        up, down = up + v, down + v - NZ
        worst = jnp.maximum(up, down)
        m = jnp.where(worst < most, i + 1, m)
        most = jnp.minimum(most, worst)
    least = (most + LANES - 1) >> 2
    for i, v in enumerate(near):
        least = jnp.maximum(least, jnp.where(i < m, v, NZ - v))
    mine = jnp.int32(0)
    for R in ROUNDS[:-1]:
        mine = mine + jnp.where(least > R, 1, 0)
    need[...] = jnp.full(need.shape, mine, jnp.int32)

    @pl.loop(0, TRI)
    def _(j):
        for k in range(3):
            at = pl.ds(pl.multiple_of((3 * j + k) * 128, 128), 128)
            wide[pl.ds(k * TRI + j, T, stride=STRIDE), :] = elem[:, at].astype(jnp.float32)
            wide2[pl.ds(k * TRI + j, RB, stride=STRIDE), :] = inv[:, at].astype(jnp.float32)

    pl.semaphore_wait(barrier, slabs - 1)
    for k in range(1, slabs):
        tell(k).start()

    leaving = []
    for bit in (NO // 2, 1):
        q = my ^ bit
        b = jnp.int32(0)
        for r in range(RB):
            src = mig[0, q * RB + r]
            b = jnp.where(src >> 1 == my, src & 1, b)
        leaving.append(b)
    for r in range(RB):
        src = mig[0, my * RB + r]
        home = src >> 1
        cls[3, r] = jnp.where(home == my, src & 1, jnp.where(home == my ^ (NO // 2), 2, 3))

    lane = lax.broadcasted_iota(jnp.int32, (1, 128), 1)
    rank = [jnp.int32(0)] * T
    fills = jnp.zeros((1, 128), jnp.int32)
    for t in range(T):
        across = shift[t] >> 4
        cls[0, t] = (across + ((z + along[t]) >> 4)) & (NX - 1)
        cls[1, t] = (across + (((z - along[t]) >> 31) & 1)) & (NX - 1)
        a = (my - shift[t]) & (NO - 1)
        fills = jnp.where(lane == (tmap[0, a * T + t] & (T - 1)), t, fills)
        for u in range(t):
            before = ((along[t] - along[u]) >> 31) & 1
            rank[u] = rank[u] + before
            rank[t] = rank[t] + 1 - before
    place[...] = fills

    goes_up = [rank[t] < m for t in range(T)]
    dist = [jnp.where(goes_up[t], along[t], NZ - along[t]) for t in range(T)]
    at_up = at_down = jnp.int32(0)
    start = []
    for t in range(T):
        start.append(jnp.where(goes_up[t], at_up, at_down))
        at_up = at_up + jnp.where(goes_up[t], dist[t], 0)
        at_down = at_down + jnp.where(goes_up[t], 0, dist[t])
        cls[2, t] = jnp.where(dist[t] == 0, 1, 0)

    for n, R in enumerate(ROUNDS):
        magic = 65536 // R + 1
        entry = jnp.zeros((1, 128), jnp.int32)
        for t in range(T):
            c, d = start[t], dist[t]
            base = jnp.where(goes_up[t], 0, LANES * R)
            last = c + d - 1
            lane1 = (last * magic) >> 16
            wraps = lane1 * R > c
            head = jnp.where(wraps, lane1 * R, c)
            moves = d > 0
            wraps = wraps & moves
            entry = jnp.where(lane == jnp.where(moves, base + head, -1), 1 + 4 * t, entry)
            entry = jnp.where(lane == jnp.where(wraps, base + c, -1), 2, entry)
            entry = jnp.where(lane == jnp.where(wraps, base + last, -1), entry + 256, entry)
            final[n, t] = jnp.where(
                moves, jnp.maximum(base + jnp.where(wraps, head - 1, last), 0), 0
            )
        route[n:n + 1, :] = entry

    @pl.loop(0, T)
    def _(t):
        tiles[t] = wide[pl.ds(pl.multiple_of(t * STRIDE, 8), ROWS), :].astype(jnp.bfloat16)

    for b in range(RB):
        own[b] = wide2[pl.ds(b * STRIDE, ROWS), :].astype(jnp.bfloat16)
    for n in range(2):
        moved[n] = own[leaving[n]]

    top = need[...]
    for k in range(1, slabs):
        tell(k).wait()
        top = jnp.maximum(top, heard[k])
    level[0, 0] = jnp.max(top)


def main_kernel(
    v, route, place, cls, final, col, tiles, own, moved, rhs, out,
    recv1, recv2, send1, send2, save, xp1, xm1, xf1, xp2, xm2, xf2, init2, stage, rowt,
    got, fac, pad0, pad1, pad2, vec, mix, it,
    zr1, zr2, zs1, zs2, xr1, xr2, xs1, xs2, mr, ms, hr, hs,
):
    R = ROUNDS[v]
    g = lax.axis_index("gx")
    slabs = lax.axis_size("gx")
    my = lax.axis_index("yz")
    x, z = my // NZ, lax.rem(my, NZ)
    line = x * NZ
    z_to = ({"yz": line + lax.rem(z + 1, NZ)}, {"yz": line + lax.rem(z + NZ - 1, NZ)})
    x_to = ({"yz": lax.rem(x + 1, NX) * NZ + z}, {"yz": lax.rem(x + NX - 1, NX) * NZ + z})
    m_to = ({"yz": lax.rem(x + NX // 2, NX) * NZ + z}, {"yz": my + 1 - 2 * lax.rem(my, 2)})
    g_to = ({"gx": lax.rem(g + 1, slabs)}, {"gx": lax.rem(g + slabs - 1, slabs)})
    pads = (pad0, pad1, pad2)

    def remote(src, dst, send, recv, to):
        return pltpu.make_async_remote_copy(
            src_ref=src, dst_ref=dst, send_sem=send, recv_sem=recv, device_id=to, device_id_type=MESH
        )

    barrier = pltpu.get_barrier_semaphore()
    greet = (*z_to, *x_to, m_to[0], *g_to)
    for to in greet:
        pl.semaphore_signal(barrier, inc=1, device_id=to, device_id_type=MESH)

    def moves():
        return [remote(moved.at[n], got.at[n], ms.at[n], mr.at[n], m_to[n]) for n in range(2)]

    for buf in (*pads, vec):
        n = buf.shape[0]
        buf[:, 0:PADX, :] = jnp.zeros((n, PADX, 128), jnp.bfloat16)
        buf[:, PADX + BS:, :] = jnp.zeros((n, PADX, 128), jnp.bfloat16)
    save[...] = jnp.zeros_like(save)
    pl.semaphore_wait(barrier, len(greet))
    for c in moves():
        c.start()

    lanes = [(d, j) for j in reversed(range(LANES)) for d in range(2)]

    def z_copy(recv, sendb, zr, zs, d, j, r):
        p = (d * LANES + j) * R + r
        k = (d * LANES + j) * 2 + (r & 1)
        return remote(sendb.at[k], recv.at[p], zs.at[k], zr.at[p], z_to[d])

    def x_first(src, xp, xm, xr, xs, t, d):
        return remote(src.at[t], (xp, xm)[d].at[t], xs.at[d * T + t], xr.at[d * T + t], x_to[d])

    def x_second(xp, xm, xf, xr, xs, t, odd):
        src = (xm if odd else xp).at[t]
        return remote(src, xf.at[t], xs.at[2 * T + t], xr.at[2 * T + t], x_to[1 if odd else 0])

    def z_start(first, recv, sendb, zr, zs):
        pend = None
        for d, j in lanes:
            k = (d * LANES + j) * 2
            sendb[k] = first(route[v, (d * LANES + j) * R] >> 2 & (T - 1))
            if pend is not None:
                pend.start()
            pend = z_copy(recv, sendb, zr, zs, d, j, 0)
        pend.start()

    def x_start(x_src, xp, xm, xf, xr, xs):
        @pl.loop(0, T)
        def _(t):
            for d in range(2):
                x_first(x_src, xp, xm, xr, xs, t, d).start()

    def rounds(first, recv, sendb, zr, zs, x_src, xp, xm, xf, xr, xs):
        @pl.loop(1, R)
        def _(r):
            for d, j in lanes:
                p = (d * LANES + j) * R + r
                z_copy(recv, sendb, zr, zs, d, j, r - 1).wait_recv()
                come = recv[p - 1]
                mode = route[v, p] & 3
                new = first(route[v, p] >> 2 & (T - 1))
                if j < LANES - 1:
                    new = lax.select(mode == 2, save[d * LANES + j + 1], new)
                new = lax.select(mode == 0, come, new)

                @pl.when(r >= 2)
                def _():
                    z_copy(recv, sendb, zr, zs, d, j, r - 2).wait_send()

                sendb[(d * LANES + j) * 2 + (r & 1)] = new
                if j > 0:
                    s = d * LANES + j
                    save[s] = lax.select(route[v, p - 1] >= 256, come, save[s])
                z_copy(recv, sendb, zr, zs, d, j, r).start()

            @pl.when(r <= T // 2)
            def _():
                t = 2 * (r - 1)
                x_first(x_src, xp, xm, xr, xs, t, 0).wait_recv()
                x_second(xp, xm, xf, xr, xs, t, False).start()
                x_first(x_src, xp, xm, xr, xs, t + 1, 1).wait_recv()
                x_second(xp, xm, xf, xr, xs, t + 1, True).start()

    def x_finish(x_src, xp, xm, xf, xr, xs):
        @pl.loop(0, T // 2)
        def _(h):
            t = 2 * h
            x_first(x_src, xp, xm, xr, xs, t, 0).wait_send()
            x_first(x_src, xp, xm, xr, xs, t, 1).wait()
            x_first(x_src, xp, xm, xr, xs, t + 1, 0).wait()
            x_first(x_src, xp, xm, xr, xs, t + 1, 1).wait_send()
            for c in (x_second(xp, xm, xf, xr, xs, t, False), x_second(xp, xm, xf, xr, xs, t + 1, True)):
                c.wait()

    def z_finish(recv, sendb, zr, zs):
        for d, j in lanes:
            last = z_copy(recv, sendb, zr, zs, d, j, R - 1)
            last.wait()
            z_copy(recv, sendb, zr, zs, d, j, R - 2).wait_send()

    def of_four(n, a, b, c, d):
        return lax.select(n == 0, a, lax.select(n == 1, b, lax.select(n == 2, c, d)))

    def product(m, v):
        f0, f1, f2 = m[0:TRI], m[TRI:2 * TRI], m[2 * TRI:]
        even = jnp.dot(
            jnp.concatenate([f0, f1], axis=1), v[PADX:, :], preferred_element_type=jnp.float32
        )
        odd = jnp.dot(
            jnp.concatenate([f1, f2], axis=1), v[:PADX + BS, :], preferred_element_type=jnp.float32
        )
        return even, odd

    def halo(s):
        b = pads[s]
        mine = b.at[RB:2 * RB, PADX:PADX + BS, :]
        return (
            remote(mine, b.at[0:RB, PADX:PADX + BS, :], hs.at[2 * s], hr.at[2 * s], g_to[0]),
            remote(mine, b.at[2 * RB:, PADX:PADX + BS, :], hs.at[2 * s + 1], hr.at[2 * s + 1], g_to[1]),
        )

    def spread(ref, r, even, odd):
        ref[pl.ds(r * BS, TRI, stride=2), :] = even
        ref[pl.ds(r * BS + 1, TRI, stride=2), :] = odd

    def begin():
        for c in moves():
            c.wait()
        for r in range(RB):
            fac[r] = of_four(cls[3, r], own[0], own[1], got[0], got[1])
            vec[r, PADX:PADX + BS, :] = rhs[r]
        for r in range(RB):
            even, odd = product(fac[r], vec[r])
            spread(it, r, even, odd)
        for r in range(RB):
            pads[0][RB + r, PADX:PADX + BS, :] = it[pl.ds(r * BS, BS), :].astype(jnp.bfloat16)
        for c in halo(0):
            c.start()

    def low(t):
        return tiles[t, HALF:, :]

    z1 = (recv1, send1, zr1, zs1)
    x1 = (tiles.at[:, 0:HALF, :], xp1, xm1, xf1, xr1, xs1)
    z_start(low, *z1)
    x_start(*x1)
    rounds(low, *z1, *x1)
    x_finish(*x1)

    @pl.loop(0, T)
    def _(t):
        init2[t] = of_four(cls[0, t], tiles[t, 0:HALF, :], xp1[t], xf1[t], xm1[t])

    def high(t):
        return init2[t]

    z2 = (recv2, send2, zr2, zs2)
    x2 = (stage, xp2, xm2, xf2, xr2, xs2)
    z_start(high, *z2)
    z_finish(*z1)

    @pl.loop(0, T)
    def _(t):
        stage[t] = lax.select(cls[2, t] == 1, tiles[t, HALF:, :], recv1[final[v, t]])

    x_start(*x2)
    begin()
    rounds(high, *z2, *x2)
    x_finish(*x2)
    z_finish(*z2)

    @pl.loop(0, T)
    def _(p):
        t = place[0, p]
        rowt[p, 0:HALF, :] = lax.select(cls[2, t] == 1, init2[t], recv2[final[v, t]])
        rowt[p, HALF:, :] = of_four(cls[1, t], stage[t], xp2[t], xf2[t], xm2[t])

    for s in range(ITERS):
        b = pads[s]
        for c in halo(s):
            c.wait()

        @pl.when(g == 0)
        def _():
            b[0:RB, PADX:PADX + BS, :] = jnp.zeros((RB, BS, 128), jnp.bfloat16)

        @pl.when(g == slabs - 1)
        def _():
            b[2 * RB:, PADX:PADX + BS, :] = jnp.zeros((RB, BS, 128), jnp.bfloat16)

        for r in range(RB):
            even = odd = jnp.zeros((TRI, 128), jnp.float32)
            for k in range(NK):
                e, o = product(rowt[r * NK + k], b[col[r, k]])
                even, odd = even + e, odd + o
            spread(mix, r, even, odd)
        for r in range(RB):
            rounded = b[RB + r, PADX:PADX + BS, :].astype(jnp.float32)
            applied = rounded + mix[pl.ds(r * BS, BS), :]
            vec[r, PADX:PADX + BS, :] = (rhs[r].astype(jnp.float32) - applied).astype(jnp.bfloat16)
        for r in range(RB):
            even, odd = product(fac[r], vec[r])
            spread(mix, r, even, odd)
        if s < ITERS - 1:
            for r in range(RB):
                new = it[pl.ds(r * BS, BS), :] + mix[pl.ds(r * BS, BS), :]
                it[pl.ds(r * BS, BS), :] = new
                pads[s + 1][RB + r, PADX:PADX + BS, :] = new.astype(jnp.bfloat16)
            for c in halo(s + 1):
                c.start()
        else:
            for r in range(RB):
                out[r] = it[pl.ds(r * BS, BS), :] + mix[pl.ds(r * BS, BS), :]


def call_main(v, route, place, cls, final, col, tiles, own, moved, rhs):
    n_pos = 2 * LANES * ROUNDS[v]
    smem = pl.BlockSpec(memory_space=pltpu.SMEM)
    vmem = pl.BlockSpec(memory_space=pltpu.VMEM)
    bf, f32 = jnp.bfloat16, jnp.float32
    half = lambda n: pltpu.VMEM((n, HALF, 128), bf)
    padded = lambda n: pltpu.VMEM((n, 2 * PADX + BS, 128), bf)
    dma = pltpu.SemaphoreType.DMA
    return pl.pallas_call(
        functools.partial(main_kernel, v),
        name="main%d" % ROUNDS[v],
        out_shape=jax.ShapeDtypeStruct((RB, BS, 128), f32),
        in_specs=[smem] * 5 + [vmem] * 4,
        out_specs=vmem,
        scratch_shapes=[
            half(n_pos), half(n_pos), half(4 * LANES), half(4 * LANES), half(2 * LANES),
            half(T), half(T), half(T), half(T), half(T), half(T), half(T), half(T),
            pltpu.VMEM((T, ROWS, 128), bf),
            pltpu.VMEM((2, ROWS, 128), bf),
            pltpu.VMEM((RB, ROWS, 128), bf),
            padded(3 * RB), padded(3 * RB), padded(3 * RB), padded(RB),
            pltpu.VMEM((RB * BS, 128), f32),
            pltpu.VMEM((RB * BS, 128), f32),
            dma((n_pos,)), dma((n_pos,)), dma((4 * LANES,)), dma((4 * LANES,)),
            dma((3 * T,)), dma((3 * T,)), dma((3 * T,)), dma((3 * T,)),
            dma((2,)), dma((2,)), dma((2 * ITERS,)), dma((2 * ITERS,)),
        ],
        compiler_params=pltpu.CompilerParams(
            collective_id=1 + v, has_side_effects=True, vmem_limit_bytes=VMEM_LIMIT
        ),
    )(route, place, cls, final, col, tiles, own, moved, rhs)


def shards(elem_tiles, inv_factor, rhs, mig_source, tile_target, col_index):
    smem = pl.BlockSpec(memory_space=pltpu.SMEM)
    vmem = pl.BlockSpec(memory_space=pltpu.VMEM)
    bf, f32, i32 = jnp.bfloat16, jnp.float32, jnp.int32
    slabs = lax.axis_size("gx")
    rounds = len(ROUNDS)
    tiles, own, moved, route, place, cls, final, level = pl.pallas_call(
        prep_kernel,
        name="prep",
        out_shape=(
            jax.ShapeDtypeStruct((T, ROWS, 128), bf),
            jax.ShapeDtypeStruct((RB, ROWS, 128), bf),
            jax.ShapeDtypeStruct((2, ROWS, 128), bf),
            jax.ShapeDtypeStruct((rounds, 128), i32),
            jax.ShapeDtypeStruct((1, 128), i32),
            jax.ShapeDtypeStruct((4, T), i32),
            jax.ShapeDtypeStruct((rounds, T), i32),
            jax.ShapeDtypeStruct((1, 1), i32),
        ),
        in_specs=[smem, smem, vmem, vmem],
        out_specs=(vmem,) * 5 + (smem,) * 3,
        scratch_shapes=[
            pltpu.VMEM((8, 128), i32),
            pltpu.VMEM((T * STRIDE, 128), f32),
            pltpu.VMEM((RB * STRIDE, 128), f32),
            pltpu.VMEM((slabs, 8, 128), i32),
            pltpu.SemaphoreType.DMA((slabs,)),
            pltpu.SemaphoreType.DMA((slabs,)),
        ],
        compiler_params=pltpu.CompilerParams(
            collective_id=0, has_side_effects=True, vmem_limit_bytes=VMEM_LIMIT
        ),
    )(tile_target, mig_source, elem_tiles, inv_factor)

    return lax.switch(
        level[0, 0],
        [functools.partial(call_main, v) for v in range(len(ROUNDS))],
        route, place, cls, final, col_index, tiles, own, moved, rhs,
    )


def solution(mesh):
    placed = (
        P(("gx", "yz"), None),
        P(("gx", "yz"), None),
        P(("gx", "yz"), None, None),
        P("gx", None),
        P("gx", None),
        P(("gx", "yz"), None),
    )
    return jax.shard_map(
        shards, mesh=mesh, in_specs=placed, out_specs=P(("gx", "yz"), None, None), check_vma=False
    )
```
